32 devices in a mesh: sweep: 2 (over x), na: 16 (over z, y, core).
Axes of the slice: x: 2, y: 2, z: 4, core: 2. Of those that a mesh axis runs over, the one named last changes fastest.
Arguments:
- hierarchy: float32 [32, 16, 2, 128, 128], P(('sweep', 'na')), parts along dimension 0, may hold values from -6 to 6
- hamiltonian: float32 [128, 128], replicated, may hold values from -0.5 to 0.5
- couplings: float32 [2, 128, 128], replicated, may hold values from -0.5 to 0.5
- damp_rates: float32 [4], P('sweep'), parts along dimension 0, may hold values from 0.5 to 2
- coef_real: float32 [4], P('sweep'), parts along dimension 0, may hold values from 0.5 to 2
- coef_imag: float32 [4], P('sweep'), parts along dimension 0, may hold values from -1 to 1
Outputs:
- evolved: float32 [32, 16, 2, 128, 128], P(('sweep', 'na')), parts along dimension 0
The draws below stay inside these ranges and needn't reach their ends.
There are 2 independent parts, one for each index of `sweep`. The reference program is written for one: setup_inputs(seed, part) draws one part's arguments, and reference() takes and returns one part's arrays. A program takes and returns all parts, laid end to end along the dimension named above; an argument that names none is the same for every part. Nothing has to cross between parts.
All inputs are finite; a program needn't handle non-finite values.
Results may differ from the reference program's by a relative error of at most 0.0001.
Values sent between devices are 32-bit elements; how exact they have to be, the bound alone decides.
No kernel may reach another device: no remote copies, remote signals or barrier semaphores. Data moves between devices by JAX's collectives and lax.ppermute only.
A program may use at most 128 MiB of HBM per device.

```python
import math
import jax
import jax.numpy as jnp
from jax import lax

M = 128
STEPS = 1
N_NA = 16


def shard_levels(own_key, dims, shards, least, top_value):
    factor_of, own = 1.0, jax.random.fold_in(own_key, 6)
    for dim, parts in shards:
        heights = jnp.exp(jax.random.uniform(jax.random.fold_in(own, dim), (parts,), jnp.float32, least / len(shards), top_value / len(shards)))
        factor_of = factor_of * jnp.repeat(heights, dims[dim] // parts).reshape([-1 if axis == dim else 1 for axis in range(len(dims))])
    return factor_of


def normal_values(key, dims, width, most, shards=(), held_as=jnp.bfloat16):
    gain = shard_levels(key, dims, shards, -0.22, 0.18) if shards else 1.0
    drawn = jax.random.normal(key, dims, jnp.float32) * width * gain
    return jnp.minimum(jnp.maximum(drawn, -most), most).astype(held_as)


def setup_inputs(seed: int = 0, part: int = 0) -> dict:
    splits = jax.random.split(jax.random.key(seed), 7)
    part_splits = jax.random.split(jax.random.fold_in(splits[6], part), 7)
    hierarchy = normal_values(part_splits[0], (N_NA, N_NA, 2, M, M), 1.0, 6.0, ((0, 16),), jnp.float32)
    hamiltonian = normal_values(splits[1], (M, M), M ** -0.5, 0.5, (), jnp.float32)
    couplings = normal_values(splits[2], (2, M, M), M ** -0.5, 0.5, (), jnp.float32)
    damp_rates = jnp.clip(jnp.exp(jax.random.uniform(part_splits[3], (2,), jnp.float32, math.log(0.5), math.log(2.0))), 0.5, 2.0)
    coef_real = jnp.clip(jnp.exp(jax.random.uniform(part_splits[4], (2,), jnp.float32, math.log(0.5), math.log(2.0))), 0.5, 2.0)
    coef_imag = jnp.clip(jax.random.uniform(part_splits[5], (2,), jnp.float32, -1.0, 1.0), -1.0, 1.0)
    return dict(hierarchy=hierarchy, hamiltonian=hamiltonian, couplings=couplings, damp_rates=damp_rates, coef_real=coef_real, coef_imag=coef_imag)


step_size = 0.02

def evolve(values, raise_one, lower_one, raise_two, lower_two, first_mode, second_mode, alive_mask, hamilton, coupled, damp_rates, coef_real, coef_imag):
    matrix_order = values.shape[-1]
    magnitude = jnp.sqrt(coef_real * coef_real + coef_imag * coef_imag)
    left_terms = [values]
    right_terms = [values]
    mode_terms = ((raise_one, lower_one, first_mode), (raise_two, lower_two, second_mode))
    for which_mode in range(2):
        raised, lowered, occupied = mode_terms[which_mode]
        raise_weight = jnp.sqrt((occupied + 1.0) * magnitude[which_mode])[..., None, None]
        lower_weight = jnp.sqrt(occupied / magnitude[which_mode])[..., None, None]
        real_coef = coef_real[which_mode]
        imag_coef = coef_imag[which_mode]
        shared_re = raise_weight * raised[..., 0, :, :]
        shared_im = raise_weight * raised[..., 1, :, :]
        direct_re = lower_weight * (real_coef * lowered[..., 0, :, :])
        direct_im = lower_weight * (real_coef * lowered[..., 1, :, :])
        cross_re = lower_weight * (imag_coef * lowered[..., 1, :, :])
        cross_im = lower_weight * (imag_coef * lowered[..., 0, :, :])
        left_terms.append(jnp.stack([shared_re + direct_re - cross_re, shared_im + direct_im + cross_im], axis=-3))
        right_terms.append(jnp.stack([shared_re + direct_re + cross_re, shared_im + direct_im - cross_im], axis=-3))
    operators = (hamilton, coupled[0], coupled[1])
    flat_shape = (-1, 2, matrix_order, matrix_order)
    left_sum = sum((jnp.einsum('ab,scbd->scad', operand, stacked.reshape(flat_shape), precision=lax.Precision.HIGHEST) for operand, stacked in zip(operators, left_terms)))
    right_sum = sum((jnp.einsum('scab,bd->scad', stacked.reshape(flat_shape), operand, precision=lax.Precision.HIGHEST) for operand, stacked in zip(operators, right_terms)))
    damping = (first_mode * damp_rates[0] + second_mode * damp_rates[1]).reshape((-1, 1, 1))
    flat_values = values.reshape(flat_shape)
    change_re = left_sum[:, 1] - right_sum[:, 1] - damping * flat_values[:, 0]
    change_im = right_sum[:, 0] - left_sum[:, 0] - damping * flat_values[:, 1]
    change = jnp.stack([change_re, change_im], axis=1).reshape(values.shape)
    return change * alive_mask[..., None, None, None]

def reference(hierarchy, hamiltonian, couplings, damp_rates, coef_real, coef_imag):
    total_slots = hierarchy.shape[0]
    hamilton = 0.5 * (hamiltonian + hamiltonian.T)
    coupled = 0.5 * (couplings + jnp.swapaxes(couplings, 1, 2))
    slot_index = jnp.arange(total_slots)
    first_mode = jnp.broadcast_to(slot_index[:, None], (total_slots, total_slots)).astype(jnp.float32)
    second_mode = jnp.broadcast_to(slot_index[None, :], (total_slots, total_slots)).astype(jnp.float32)
    alive_mask = (first_mode + second_mode <= total_slots - 1).astype(jnp.float32)

    def derivative(values):
        pad_first = jnp.zeros_like(values[:1])
        pad_second = jnp.zeros_like(values[:, :1])
        raise_one = jnp.concatenate([values[1:], pad_first], 0)
        lower_one = jnp.concatenate([pad_first, values[:-1]], 0)
        raise_two = jnp.concatenate([values[:, 1:], pad_second], 1)
        lower_two = jnp.concatenate([pad_second, values[:, :-1]], 1)
        return evolve(values, raise_one, lower_one, raise_two, lower_two, first_mode, second_mode, alive_mask, hamilton, coupled, damp_rates, coef_real, coef_imag)
    values = hierarchy * alive_mask[..., None, None, None]
    for step_index in range(STEPS):
        middle = values + 0.5 * step_size * derivative(values)
        values = values + step_size * derivative(middle)
    return values
```

```python
import functools

import jax
import jax.numpy as jnp
from jax import lax
from jax.experimental import pallas as pl
from jax.experimental.pallas import tpu as pltpu
from jax.sharding import PartitionSpec as P

step_size = 0.02
f32, bf16 = jnp.float32, jnp.bfloat16
FIELDS = 9


def split(x):
    hi = x.astype(bf16)
    return hi, (x - hi.astype(f32)).astype(bf16)


def dot(a, b):
    return jnp.dot(a, b, preferred_element_type=f32)


def derivative(center, plus, minus, above, below, weights, left_ops, right_ops):
    size = center[0].shape[0]
    pr, pi, mr, mi, ur, dr, di, gamma = weights
    a_re = pr * plus[0] + mr * minus[0]
    a_im = pr * plus[1] + mr * minus[1]
    b_re = pi * plus[1] + mi * minus[1]
    b_im = pi * plus[0] + mi * minus[0]
    c_re = ur * above[0] + dr * below[0]
    c_im = ur * above[1] + dr * below[1]
    d_re = di * below[1]
    d_im = di * below[0]
    re_h, re_l = split(center[0])
    im_h, im_l = split(center[1])
    left = [(re_h, re_l, im_h, im_l)]
    right = [(re_h, re_l, im_h, im_l)]
    for s_re, s_im, x_re, x_im in ((a_re, a_im, b_re, b_im), (c_re, c_im, d_re, d_im)):
        left.append((*split(s_re - x_re), *split(s_im + x_im)))
        right.append((*split(s_re + x_re), *split(s_im - x_im)))
    cat = jnp.concatenate
    left_h = cat([cat([e[0], e[2]], 1) for e in left], 0)
    left_l = cat([cat([e[1], e[3]], 1) for e in left], 0)
    right_h = cat([cat([e[0] for e in right], 1), cat([e[2] for e in right], 1)], 0)
    right_l = cat([cat([e[1] for e in right], 1), cat([e[3] for e in right], 1)], 0)
    twice = dot(left_ops, left_h)
    ls = twice[:size] + twice[size:] + dot(left_ops[:size], left_l)
    twice = dot(right_h, right_ops)
    rs = twice[:, :size] + twice[:, size:] + dot(right_l, right_ops[:, :size])
    change_re = ls[:, size:] - rs[size:] - gamma * center[0]
    change_im = rs[:size] - ls[:, :size] - gamma * center[1]
    return change_re, change_im


def stage_kernel(spec, ints, table, left_ref, right_ref, *refs):
    slots, pieces, lo, hi, first, last = spec
    refs = list(refs)
    own_hbm, partner_hbm = refs.pop(0), refs.pop(0)
    fars = [[refs.pop(0) for _ in pieces] for _ in range(4)]
    carry_hbm = out_hbm = None
    if not first:
        carry_hbm = refs.pop(0)
        refs.pop(0)
    out_hbm = refs.pop(0)
    carry_out = None if last else refs.pop(0)
    own, partner, two, one, mid, out, sems = refs
    base = max(lo - 2, 0)
    mid_base = max(lo - 3, 0)
    out_base = max(lo - 2, 0)
    near_end = slots if last else hi
    mid_end = slots + 1 if last else hi - 1
    out_end = slots if last else hi - 2
    copies = []

    def fetch(src, dst):
        copy = pltpu.make_async_copy(src, dst, sems.at[len(copies)])
        copy.start()
        copies.append(copy)

    near = near_end - base
    fetch(own_hbm.at[pl.ds(base, near)], own.at[pl.ds(0, near)])
    fetch(partner_hbm.at[pl.ds(base, near)], partner.at[pl.ds(0, near)])
    for which in range(4):
        target = (two, one)[which // 2].at[which % 2]
        for ref, (start, stop) in zip(fars[which], pieces):
            begin = max(start, base)
            fetch(
                ref.at[pl.ds(begin - start, stop - begin)],
                target.at[pl.ds(begin - base, stop - begin)],
            )
    if not first:
        fetch(carry_hbm, mid.at[:, pl.ds(0, 2)])
    for copy in copies:
        copy.wait()
    plus_two = ints[0]
    far_one = ints[1]
    far_last = hi - 1 - base
    near_last = near_end - 1 - base

    def pair(ref, *index):
        return ref[(*index, 0)], ref[(*index, 1)]

    def body(level, _):
        def clamp(i, top):
            return jnp.clip(i - base, 0, top)

        def weights(row, at):
            offset = (row * (slots + 1) + at) * FIELDS
            return [table[offset + k] for k in range(FIELDS)]

        here_n, up_n, down_n = [clamp(level + s, near_last) for s in (0, 1, -1)]
        here_f, up_f, down_f = [clamp(level + s, far_last) for s in (0, 1, -1)]
        mine = pair(own, here_n)
        other = pair(partner, here_n)
        far = pair(one, far_one, here_f)
        rows = (
            (far, mine, pair(two, 1 - plus_two, here_f), pair(one, far_one, up_f), pair(one, far_one, down_f)),
            (mine, other, far, pair(own, up_n), pair(own, down_n)),
            (other, pair(two, plus_two, here_f), mine, pair(partner, up_n), pair(partner, down_n)),
        )
        left_ops, right_ops = left_ref[...], right_ref[...]
        at_mid = level - mid_base
        for row in (1, 0, 2):
            *w, keep = weights(row, level)
            center = rows[row][0]
            change = derivative(*rows[row], w, left_ops, right_ops)
            for part in range(2):
                mid[row, at_mid, part] = keep * (center[part] + 0.5 * step_size * change[part])
        below = jnp.maximum(level - 1, 0)
        *w, keep = weights(1, below)
        at = below - mid_base
        change = derivative(
            pair(mid, 1, at),
            pair(mid, 2, at),
            pair(mid, 0, at),
            pair(mid, 1, at + 1),
            pair(mid, 1, jnp.maximum(at - 1, 0)),
            w,
            left_ops,
            right_ops,
        )
        old = pair(own, clamp(below, near_last))
        for part in range(2):
            out[below - out_base, part] = keep * (old[part] + step_size * change[part])
        return 0

    lax.fori_loop(max(lo - 1, 0), mid_end, body, 0)
    done = [
        pltpu.make_async_copy(
            out.at[pl.ds(0, out_end - out_base)],
            out_hbm.at[pl.ds(out_base, out_end - out_base)],
            sems.at[0],
        )
    ]
    if not last:
        done.append(
            pltpu.make_async_copy(
                mid.at[:, pl.ds(hi - 3 - mid_base, 2)], carry_out, sems.at[1]
            )
        )
    for copy in done:
        copy.start()
    for copy in done:
        copy.wait()


def stage(slots, order, cuts, lo, hi, ints, table, left_ops, right_ops, own, partner, fars, carry, out):
    first, last = lo == 0, hi == slots - 1
    base = max(lo - 2, 0)
    used = [i for i, (a, b) in enumerate(cuts) if b > base and a < hi]
    pieces = [cuts[i] for i in used]
    matrix = (2, order, order)
    operands = [ints, table, left_ops, right_ops, own, partner]
    for group in fars:
        operands += [group[i] for i in used]
    aliases = {}
    if not first:
        operands += [carry, out]
        aliases = {len(operands) - 1: 0}
    width = (slots if last else hi) - base
    mids = (slots + 1 if last else hi - 1) - max(lo - 3, 0)
    outs = (slots if last else hi - 2) - base
    smem, vmem = pl.BlockSpec(memory_space=pltpu.SMEM), pl.BlockSpec(memory_space=pltpu.VMEM)
    hbm = pl.BlockSpec(memory_space=pl.ANY)
    out_shape = [jax.ShapeDtypeStruct((slots, *matrix), f32)]
    if not last:
        out_shape.append(jax.ShapeDtypeStruct((3, 2, *matrix), f32))
    cells = 4 * (mids - 2)
    results = pl.pallas_call(
        functools.partial(stage_kernel, (slots, pieces, lo, hi, first, last)),
        out_shape=out_shape,
        in_specs=[smem, smem, vmem, vmem] + [hbm] * (len(operands) - 4),
        out_specs=[hbm] * len(out_shape),
        scratch_shapes=[
            pltpu.VMEM((width, *matrix), f32),
            pltpu.VMEM((width, *matrix), f32),
            pltpu.VMEM((2, width, *matrix), f32),
            pltpu.VMEM((2, width, *matrix), f32),
            pltpu.VMEM((3, mids + 1, *matrix), f32),
            pltpu.VMEM((outs, *matrix), f32),
            pltpu.SemaphoreType.DMA((3 + 4 * len(pieces),)),
        ],
        input_output_aliases=aliases,
        cost_estimate=pl.CostEstimate(
            flops=cells * 72 * order**3, bytes_accessed=cells * 8 * order**2, transcendentals=0
        ),
        name=f"stage_{lo}",
    )(*operands)
    return results


def weight_table(slots, position, toward, damp_rates, coef_real, coef_imag):
    magnitude = jnp.sqrt(coef_real * coef_real + coef_imag * coef_imag)
    row = (position + toward * (jnp.arange(3) - 1))[:, None]
    level = jnp.arange(slots + 1)[None, :]

    def alive(a, b):
        return ((a >= 0) & (b >= 0) & (a + b <= slots - 1)).astype(f32)

    here = alive(row, level)
    one = jnp.maximum(row, 0).astype(f32)
    two = level.astype(f32)
    up_one = jnp.sqrt((one + 1.0) * magnitude[0])
    down_one = jnp.sqrt(one / magnitude[0])
    up_two = jnp.sqrt((two + 1.0) * magnitude[1])
    down_two = jnp.sqrt(two / magnitude[1])
    raised = here * alive(row + 1, level)
    lowered = here * alive(row - 1, level)
    upper = (up_one * raised, jnp.zeros_like(here))
    lower = (down_one * coef_real[0] * lowered, down_one * coef_imag[0] * lowered)
    forward = toward > 0
    plus = [jnp.where(forward, a, b) for a, b in zip(upper, lower)]
    minus = [jnp.where(forward, b, a) for a, b in zip(upper, lower)]
    above = up_two * here * alive(row, level + 1)
    lowered = here * alive(row, level - 1)
    fields = [
        *plus,
        *minus,
        above,
        down_two * coef_real[1] * lowered,
        down_two * coef_imag[1] * lowered,
        one * damp_rates[0] + two * damp_rates[1],
        here,
    ]
    return jnp.stack([jnp.broadcast_to(f, here.shape) for f in fields], -1).reshape(-1)


def cut_points(slots):
    top = slots - 1
    points = sorted({0, *[round(top * k / 15) for k in (2, 5, 9, 12)], top})
    return list(zip(points[:-1], points[1:]))


def per_device(hierarchy, hamiltonian, couplings, damp_rates, coef_real, coef_imag):
    slots, order = hierarchy.shape[1], hierarchy.shape[-1]
    position = lax.axis_index("na")
    core, side = position % 2, (position // 2) % 2
    toward = 1 - 2 * core
    operators = [0.5 * (m + m.T) for m in (hamiltonian, couplings[0], couplings[1])]
    parts = []
    for m in operators:
        coarse = lax.reduce_precision(m, 8, 7)
        parts.append((coarse.astype(bf16), (m - coarse).astype(bf16)))
    left_ops = jnp.concatenate(
        [jnp.concatenate([p[k] for p in parts], 1) for k in range(2)], 0
    )
    right_ops = jnp.concatenate(
        [jnp.concatenate([p[k] for p in parts], 0) for k in range(2)], 1
    )
    table = weight_table(slots, position, toward, damp_rates, coef_real, coef_imag)
    ints = jnp.stack([core ^ side, 1 - (core ^ side)]).astype(jnp.int32)
    own = hierarchy[0]
    cuts = cut_points(slots)
    devices = range(slots)
    partner = lax.ppermute(own, "na", [(d, d ^ 1) for d in devices])
    pair_far, next_far, pair_near, next_near = [], [], [], []
    for lo, hi in cuts:
        piece = own[lo:hi]
        sent = [d for d in devices if d + lo <= slots - 1 - 2 * (d == 0)]
        pair = lax.ppermute(piece, "na", [(d, d ^ 2) for d in sent])
        handed = [(d, d + 4) for d in devices if not d & 2 and d + 4 < slots and lo + d + 3 <= slots]
        handed += [(d, d - 4) for d in devices if d & 2 and d >= 4 and lo + d - 2 <= slots - 1]
        pair_far.append(pair)
        pair_near.append(lax.ppermute(pair, "na", [(d, d ^ 1) for d in devices if (d ^ d >> 1) & 1 == 0]))
        if handed:
            passed = lax.ppermute(pair, "na", handed)
            next_far.append(passed)
            next_near.append(
                lax.ppermute(passed, "na", [(d, d ^ 1) for d in devices if (d ^ d >> 1) & 1])
            )
        else:
            next_far.append(jnp.zeros_like(pair))
            next_near.append(jnp.zeros_like(pair))
    fars = (pair_far, next_far, pair_near, next_near)
    bounds = [0] + [hi for _, hi in cuts[1:]]
    carry = out = None
    for lo, hi in zip(bounds[:-1], bounds[1:]):
        results = stage(
            slots, order, cuts, lo, hi, ints, table, left_ops, right_ops, own, partner, fars, carry, out
        )
        out, carry = results[0], results[-1]
    return out[None]


def solution(mesh):
    in_specs = (
        P(("sweep", "na"), None, None, None, None),
        P(),
        P(),
        P("sweep"),
        P("sweep"),
        P("sweep"),
    )
    out_specs = P(("sweep", "na"), None, None, None, None)
    return jax.shard_map(
        per_device, mesh=mesh, in_specs=in_specs, out_specs=out_specs, check_vma=False
    )
```

```python
import functools

import jax
import numpy as np
import jax.numpy as jnp
from jax import lax
from jax.experimental import pallas as pl
from jax.experimental.pallas import tpu as pltpu
from jax.sharding import PartitionSpec as P

step_size = 0.02
f32, bf16 = jnp.float32, jnp.bfloat16


def split(x):
    hi = x.astype(bf16)
    return hi, (x - hi.astype(f32)).astype(bf16)


def dot(a, b):
    return jnp.dot(a, b, preferred_element_type=f32)


def derivative(center, plus, minus, above, below, weights, left_ops, right_ops):
    size = center[0].shape[0]
    pr, pi, mr, mi, ur, dr, di, gamma = weights
    a_re = pr * plus[0] + mr * minus[0]
    a_im = pr * plus[1] + mr * minus[1]
    b_re = pi * plus[1] + mi * minus[1]
    b_im = pi * plus[0] + mi * minus[0]
    c_re = ur * above[0] + dr * below[0]
    c_im = ur * above[1] + dr * below[1]
    d_re = di * below[1]
    d_im = di * below[0]
    re_h, re_l = split(center[0])
    im_h, im_l = split(center[1])
    left = [(re_h, re_l, im_h, im_l)]
    right = [(re_h, re_l, im_h, im_l)]
    for s_re, s_im, x_re, x_im in ((a_re, a_im, b_re, b_im), (c_re, c_im, d_re, d_im)):
        left.append((*split(s_re - x_re), *split(s_im + x_im)))
        right.append((*split(s_re + x_re), *split(s_im - x_im)))
    cat = jnp.concatenate
    left_h = cat([cat([e[0], e[2]], 1) for e in left], 0)
    left_l = cat([cat([e[1], e[3]], 1) for e in left], 0)
    right_h = cat([cat([e[0] for e in right], 1), cat([e[2] for e in right], 1)], 0)
    right_l = cat([cat([e[1] for e in right], 1), cat([e[3] for e in right], 1)], 0)
    twice = dot(left_ops, left_h)
    ls = twice[:size] + twice[size:] + dot(left_ops[:size], left_l)
    twice = dot(right_h, right_ops)
    rs = twice[:, :size] + twice[:, size:] + dot(right_l, right_ops[:, :size])
    change_re = ls[:, size:] - rs[size:] - gamma * center[0]
    change_im = rs[:size] - ls[:, :size] - gamma * center[1]
    return change_re, change_im


def scalars(ints, roots, rates, slots, row, level):
    toward = ints[1]
    first = ints[0] + toward * (row - 1)
    inside = jnp.logical_and(first >= 0, first + level <= slots - 1)
    here = jnp.where(inside, 1.0, 0.0)
    raised = jnp.where(jnp.logical_and(inside, first + level <= slots - 2), 1.0, 0.0)
    safe = jnp.maximum(first, 0)
    up = raised * roots[safe + 1] * rates[0]
    low = here * roots[safe]
    low_re, low_im = low * rates[1], low * rates[2]
    onward = toward > 0
    plus = jnp.where(onward, up, low_re), jnp.where(onward, 0.0, low_im)
    minus = jnp.where(onward, low_re, up), jnp.where(onward, low_im, 0.0)
    above = raised * roots[level + 1] * rates[4]
    below = here * roots[level]
    count = slots + 2
    gamma = roots[count + safe] * rates[3] + roots[count + level] * rates[7]
    weights = (plus[0], plus[1], minus[0], minus[1], above, below * rates[5], below * rates[6], gamma)
    return weights, here


def pair(ref, *index):
    return ref[(*index, 0)], ref[(*index, 1)]


def top_kernel(slots, ints, roots, rates, left_ref, right_ref, own_hbm, partner_hbm, top_out, out_hbm, own, partner, top, out, sems):
    base = slots - 3
    copies = [
        pltpu.make_async_copy(own_hbm.at[pl.ds(base, 3)], own, sems.at[0]),
        pltpu.make_async_copy(partner_hbm.at[pl.ds(base, 3)], partner, sems.at[1]),
    ]
    for copy in copies:
        copy.start()
    for copy in copies:
        copy.wait()
    ops = left_ref[...], right_ref[...]
    values = []
    for row, (mine, other) in ((1, (own, partner)), (2, (partner, own))):
        for at in (1, 2):
            center, near = pair(mine, at), pair(other, at)
            plus, minus = (near, center) if row == 1 else (center, near)
            weights, here = scalars(ints, roots, rates, slots, row, base + at)
            weights = list(weights)
            away = 2 if row == 1 else 0
            weights[away] = weights[away + 1] = 0.0
            change = derivative(center, plus, minus, pair(mine, min(at + 1, 2)), pair(mine, at - 1), weights, *ops)
            value = [here * (c + 0.5 * step_size * d) for c, d in zip(center, change)]
            values.append(value)
            for part in range(2):
                top[row, at - 1, part] = value[part]
    for at in (0, 1):
        for part in range(2):
            top[0, at, part] = jnp.zeros_like(values[0][0])
    weights, here = scalars(ints, roots, rates, slots, 1, slots - 1)
    change = derivative(values[1], values[3], values[1], values[1], values[0], weights, *ops)
    for part in range(2):
        out[0, part] = here * (own[2, part] + step_size * change[part])
    copies = [
        pltpu.make_async_copy(top, top_out, sems.at[0]),
        pltpu.make_async_copy(out, out_hbm.at[pl.ds(slots - 1, 1)], sems.at[1]),
    ]
    for copy in copies:
        copy.start()
    for copy in copies:
        copy.wait()


def stage_kernel(spec, ints, roots, rates, left_ref, right_ref, *refs):
    slots, pieces, lo, hi, first, last = spec
    refs = list(refs)
    own_hbm, partner_hbm = refs.pop(0), refs.pop(0)
    fars = [[refs.pop(0) for _ in pieces] for _ in range(4)]
    carry_hbm = None if first else refs.pop(0)
    top_hbm = refs.pop(0) if last else None
    refs.pop(0)
    out_hbm = refs.pop(0)
    carry_out = None if last else refs.pop(0)
    own, partner, two, one, mid, out, sems, late, out_sems = refs
    base = max(lo - 2, 0)
    mid_base = max(lo - 3, 0)
    near_end = hi + 1 if last else hi
    begin, mid_end = max(lo - 1, 0), hi - 1
    out_end = slots - 1 if last else hi - 2

    def fetches(level):
        at = level - base
        found = [(own_hbm.at[level], own.at[at]), (partner_hbm.at[level], partner.at[at])]
        for which in range(4):
            target = (two, one)[which // 2].at[which % 2]
            for ref, (start, stop) in zip(fars[which], pieces):
                if start <= level < stop:
                    found.append((ref.at[level - start], target.at[at]))
        return [
            pltpu.make_async_copy(src, dst, sems.at[at, k]) for k, (src, dst) in enumerate(found)
        ]

    extra = []
    if not first:
        extra.append(pltpu.make_async_copy(carry_hbm, mid.at[:, pl.ds(0, 2)], late.at[0]))
    if last:
        extra.append(
            pltpu.make_async_copy(top_hbm, mid.at[:, pl.ds(slots - 2 - mid_base, 2)], late.at[1])
        )
    levels = {level: fetches(level) for level in range(base, near_end)}
    for level in range(base, min(begin + 2, near_end)):
        for copy in levels[level]:
            copy.start()
    for copy in extra:
        copy.start()
    for level in range(min(begin + 2, near_end), near_end):
        for copy in levels[level]:
            copy.start()
    for level in range(base, begin + 1):
        for copy in levels[level]:
            copy.wait()
    for copy in extra:
        copy.wait()
    plus_two, far_one = ints[2], ints[3]
    far_last = hi - 1 - base
    near_last = near_end - 1 - base
    near_count = 6

    def send(level):
        at = level - base
        return pltpu.make_async_copy(out.at[at], out_hbm.at[level], out_sems.at[at])

    def body(level, with_mid=True):
        def clamp(i, top):
            return jnp.clip(i - base, 0, top)

        ops = left_ref[...], right_ref[...]
        below = jnp.maximum(level - 1, 0)
        at = below - mid_base
        here_mid = [pair(mid, row, at) for row in range(3)]
        down_mid = pair(mid, 1, jnp.maximum(at - 1, 0))
        if with_mid:
            here, up_n, down_n = [clamp(level + s, near_last) for s in (0, 1, -1)]
            up_f = clamp(level + 1, far_last)
            mine = pair(own, here)
            other = pair(partner, here)
            far = pair(one, far_one, here)
            rows = (
                (far, mine, pair(two, 1 - plus_two, here), pair(one, far_one, up_f), pair(one, far_one, down_n)),
                (mine, other, far, pair(own, up_n), pair(own, down_n)),
                (other, pair(two, plus_two, here), mine, pair(partner, up_n), pair(partner, down_n)),
            )
            values = {}
            for row in (1, 0, 2):
                weights, inside = scalars(ints, roots, rates, slots, row, level)
                change = derivative(*rows[row], weights, *ops)
                values[row] = [
                    inside * (c + 0.5 * step_size * d) for c, d in zip(rows[row][0], change)
                ]
            up_mid = values[1]
        else:
            up_mid = pair(mid, 1, at + 1)
        weights, inside = scalars(ints, roots, rates, slots, 1, below)
        change = derivative(here_mid[1], here_mid[2], here_mid[0], up_mid, down_mid, weights, *ops)
        old = pair(own, clamp(below, near_last))
        for part in range(2):
            out[below - base, part] = inside * (old[part] + step_size * change[part])
        if with_mid:
            for row in range(3):
                for part in range(2):
                    mid[row, level - mid_base, part] = values[row][part]

    def step(level, _):
        @pl.when(level + 1 < near_end)
        def _():
            at = level + 1 - base
            for k, (hbm, ref) in enumerate(((own_hbm, own), (partner_hbm, partner))):
                pltpu.make_async_copy(hbm.at[level + 1], ref.at[at], sems.at[at, k]).wait()

        @pl.when(level + 1 < hi)
        def _():
            at = level + 1 - base
            for k in range(4):
                target = (two, one)[k // 2].at[k % 2]
                pltpu.make_async_copy(own_hbm.at[level + 1], target.at[at], sems.at[at, 2 + k]).wait()

        body(level)

        @pl.when(level >= 1)
        def _():
            send(level - 1).start()

        return 0

    lax.fori_loop(begin, mid_end, step, 0)
    if last:

        def close(level, _):
            body(level, False)
            send(level - 1).start()
            return 0

        for level in range(mid_end + 1, near_end):
            for copy in levels[level][: 2 if level >= hi else near_count]:
                copy.wait()
        lax.fori_loop(mid_end, slots, close, 0)
    else:
        keep = pltpu.make_async_copy(mid.at[:, pl.ds(hi - 3 - mid_base, 2)], carry_out, late.at[0])
        keep.start()
        keep.wait()
    for level in range(max(lo - 2, 0), out_end):
        send(level).wait()


def specs():
    return (
        pl.BlockSpec(memory_space=pltpu.SMEM),
        pl.BlockSpec(memory_space=pltpu.VMEM),
        pl.BlockSpec(memory_space=pl.ANY),
    )


def top_stage(slots, order, common, own, partner):
    smem, vmem, hbm = specs()
    matrix = (2, order, order)
    return pl.pallas_call(
        functools.partial(top_kernel, slots),
        out_shape=[
            jax.ShapeDtypeStruct((3, 2, *matrix), f32),
            jax.ShapeDtypeStruct((slots, *matrix), f32),
        ],
        in_specs=[smem] * 3 + [vmem] * 2 + [hbm] * 2,
        out_specs=[hbm] * 2,
        scratch_shapes=[
            pltpu.VMEM((3, *matrix), f32),
            pltpu.VMEM((3, *matrix), f32),
            pltpu.VMEM((3, 2, *matrix), f32),
            pltpu.VMEM((1, *matrix), f32),
            pltpu.SemaphoreType.DMA((2,)),
        ],
        cost_estimate=pl.CostEstimate(
            flops=5 * 72 * order**3, bytes_accessed=13 * 8 * order**2, transcendentals=0
        ),
        name="top",
    )(*common, own, partner)


def stage(slots, order, cuts, lo, hi, common, own, partner, fars, carry, top, out):
    first, last = lo == 0, hi == slots - 1
    base = max(lo - 2, 0)
    used = [i for i, (a, b) in enumerate(cuts) if b > base and a < hi]
    pieces = [cuts[i] for i in used]
    matrix = (2, order, order)
    operands = [*common, own, partner]
    for group in fars:
        operands += [group[i] for i in used]
    if not first:
        operands.append(carry)
    if last:
        operands.append(top)
    operands.append(out)
    width = (hi + 1 if last else hi) - base
    mids = (slots if last else hi - 1) - max(lo - 3, 0)
    smem, vmem, hbm = specs()
    out_shape = [jax.ShapeDtypeStruct((slots, *matrix), f32)]
    if not last:
        out_shape.append(jax.ShapeDtypeStruct((3, 2, *matrix), f32))
    cells = 4 * (hi - lo)
    return pl.pallas_call(
        functools.partial(stage_kernel, (slots, pieces, lo, hi, first, last)),
        out_shape=out_shape,
        in_specs=[smem] * 3 + [vmem] * 2 + [hbm] * (len(operands) - 5),
        out_specs=[hbm] * len(out_shape),
        scratch_shapes=[
            pltpu.VMEM((width, *matrix), f32),
            pltpu.VMEM((width, *matrix), f32),
            pltpu.VMEM((2, width, *matrix), f32),
            pltpu.VMEM((2, width, *matrix), f32),
            pltpu.VMEM((3, mids, *matrix), f32),
            pltpu.VMEM((width, *matrix), f32),
            pltpu.SemaphoreType.DMA((width, 6)),
            pltpu.SemaphoreType.DMA((2,)),
            pltpu.SemaphoreType.DMA((width,)),
        ],
        input_output_aliases={len(operands) - 1: 0},
        cost_estimate=pl.CostEstimate(
            flops=cells * 72 * order**3, bytes_accessed=cells * 8 * order**2, transcendentals=0
        ),
        name=f"stage_{lo}",
    )(*operands)


def cut_points(slots):
    top = slots - 1
    points = sorted({0, *[round(top * k / 15) for k in (2, 6, 10)], top - 2, top})
    return list(zip(points[:-1], points[1:]))


def per_device(hierarchy, hamiltonian, couplings, damp_rates, coef_real, coef_imag):
    slots, order = hierarchy.shape[1], hierarchy.shape[-1]
    position = lax.axis_index("na")
    core, side = position % 2, (position // 2) % 2
    toward = 1 - 2 * core
    operators = [0.5 * (m + m.T) for m in (hamiltonian, couplings[0], couplings[1])]
    parts = []
    for m in operators:
        coarse = lax.reduce_precision(m, 8, 7)
        parts.append((coarse.astype(bf16), (m - coarse).astype(bf16)))
    left_ops = jnp.concatenate(
        [jnp.concatenate([p[k] for p in parts], 1) for k in range(2)], 0
    )
    right_ops = jnp.concatenate(
        [jnp.concatenate([p[k] for p in parts], 0) for k in range(2)], 1
    )
    root = jnp.sqrt(jnp.sqrt(coef_real * coef_real + coef_imag * coef_imag))
    rates = jnp.stack([root, coef_real / root, coef_imag / root, damp_rates], 1).reshape(-1)
    counts = np.arange(slots + 2)
    roots = jnp.asarray(np.concatenate([np.sqrt(counts), counts]).astype(np.float32))
    ints = jnp.stack([position, toward, core ^ side, 1 - (core ^ side)]).astype(jnp.int32)
    common = (ints, roots, rates, left_ops, right_ops)
    own = hierarchy[0]
    cuts = cut_points(slots)
    devices = range(slots)
    partner = lax.ppermute(own, "na", [(d, d ^ 1) for d in devices])
    pair_far, next_far, pair_near, next_near = [], [], [], []
    for lo, hi in cuts:
        piece = own[lo:hi]
        sent = [d for d in devices if d + lo <= slots - 1 - 2 * (d == 0)]
        if len(pair_far) >= 2:
            piece, _ = lax.optimization_barrier((piece, pair_far[-2]))
        pair = lax.ppermute(piece, "na", [(d, d ^ 2) for d in sent])
        handed = [(d, d + 4) for d in devices if not d & 2 and d + 4 < slots and lo + d + 3 <= slots]
        handed += [(d, d - 4) for d in devices if d & 2 and d >= 4 and lo + d - 2 <= slots - 1]
        pair_far.append(pair)
        pair_near.append(lax.ppermute(pair, "na", [(d, d ^ 1) for d in devices if (d ^ d >> 1) & 1 == 0]))
        if handed:
            passed = lax.ppermute(pair, "na", handed)
            next_far.append(passed)
            next_near.append(
                lax.ppermute(passed, "na", [(d, d ^ 1) for d in devices if (d ^ d >> 1) & 1])
            )
        else:
            next_far.append(jnp.zeros_like(pair))
            next_near.append(jnp.zeros_like(pair))
    fars = (pair_far, next_far, pair_near, next_near)
    bounds = [0] + [hi for _, hi in cuts[1:]]
    top, out = top_stage(slots, order, common, own, partner)
    carry = None
    for lo, hi in zip(bounds[:-1], bounds[1:]):
        results = stage(
            slots, order, cuts, lo, hi, common, own, partner, fars, carry, top, out
        )
        out, carry = results[0], results[-1]
    return out[None]


def solution(mesh):
    in_specs = (
        P(("sweep", "na"), None, None, None, None),
        P(),
        P(),
        P("sweep"),
        P("sweep"),
        P("sweep"),
    )
    out_specs = P(("sweep", "na"), None, None, None, None)
    return jax.shard_map(
        per_device, mesh=mesh, in_specs=in_specs, out_specs=out_specs, check_vma=False
    )
```

```python
import functools

import jax
import numpy as np
import jax.numpy as jnp
from jax import lax
from jax.experimental import pallas as pl
from jax.experimental.pallas import tpu as pltpu
from jax.sharding import PartitionSpec as P

step_size = 0.02
f32, bf16 = jnp.float32, jnp.bfloat16


def split(x):
    hi = x.astype(bf16)
    return hi, (x - hi.astype(f32)).astype(bf16)


def dot(a, b):
    return jnp.dot(a, b, preferred_element_type=f32)


def derivative(center, plus, minus, above, below, weights, left_ops, right_ops):
    size = center[0].shape[0]
    pr, pi, mr, mi, ur, dr, di, gamma = weights
    a_re = pr * plus[0] + mr * minus[0]
    a_im = pr * plus[1] + mr * minus[1]
    b_re = pi * plus[1] + mi * minus[1]
    b_im = pi * plus[0] + mi * minus[0]
    c_re = ur * above[0] + dr * below[0]
    c_im = ur * above[1] + dr * below[1]
    d_re = di * below[1]
    d_im = di * below[0]
    re_h, re_l = split(center[0])
    im_h, im_l = split(center[1])
    left = [(re_h, re_l, im_h, im_l)]
    right = [(re_h, re_l, im_h, im_l)]
    for s_re, s_im, x_re, x_im in ((a_re, a_im, b_re, b_im), (c_re, c_im, d_re, d_im)):
        left.append((*split(s_re - x_re), *split(s_im + x_im)))
        right.append((*split(s_re + x_re), *split(s_im - x_im)))
    cat = jnp.concatenate
    left_h = cat([cat([e[0], e[2]], 1) for e in left], 0)
    left_l = cat([cat([e[1], e[3]], 1) for e in left], 0)
    right_h = cat([cat([e[0] for e in right], 1), cat([e[2] for e in right], 1)], 0)
    right_l = cat([cat([e[1] for e in right], 1), cat([e[3] for e in right], 1)], 0)
    twice = dot(left_ops, left_h)
    ls = twice[:size] + twice[size:] + dot(left_ops[:size], left_l)
    twice = dot(right_h, right_ops)
    rs = twice[:, :size] + twice[:, size:] + dot(right_l, right_ops[:, :size])
    change_re = ls[:, size:] - rs[size:] - gamma * center[0]
    change_im = rs[:size] - ls[:, :size] - gamma * center[1]
    return change_re, change_im


def scalars(ints, roots, rates, slots, row, level):
    toward = ints[1]
    first = ints[0] + toward * (row - 1)
    inside = jnp.logical_and(first >= 0, first + level <= slots - 1)
    here = jnp.where(inside, 1.0, 0.0)
    raised = jnp.where(jnp.logical_and(inside, first + level <= slots - 2), 1.0, 0.0)
    safe = jnp.maximum(first, 0)
    up = raised * roots[safe + 1] * rates[0]
    low = here * roots[safe]
    low_re, low_im = low * rates[1], low * rates[2]
    onward = toward > 0
    plus = jnp.where(onward, up, low_re), jnp.where(onward, 0.0, low_im)
    minus = jnp.where(onward, low_re, up), jnp.where(onward, low_im, 0.0)
    above = raised * roots[level + 1] * rates[4]
    below = here * roots[level]
    count = slots + 2
    gamma = roots[count + safe] * rates[3] + roots[count + level] * rates[7]
    weights = (plus[0], plus[1], minus[0], minus[1], above, below * rates[5], below * rates[6], gamma)
    return weights, here


def pair(ref, *index):
    return ref[(*index, 0)], ref[(*index, 1)]


def top_kernel(slots, ints, roots, rates, left_ref, right_ref, own_all, partner_all, top, out_hbm, out, sems):
    base = slots - 3
    own, partner = own_all.at[pl.ds(base, 3)], partner_all.at[pl.ds(base, 3)]
    ops = left_ref[...], right_ref[...]
    values = []
    for row, (mine, other) in ((1, (own, partner)), (2, (partner, own))):
        for at in (1, 2):
            center, near = pair(mine, at), pair(other, at)
            plus, minus = (near, center) if row == 1 else (center, near)
            weights, here = scalars(ints, roots, rates, slots, row, base + at)
            weights = list(weights)
            away = 2 if row == 1 else 0
            weights[away] = weights[away + 1] = 0.0
            change = derivative(center, plus, minus, pair(mine, min(at + 1, 2)), pair(mine, at - 1), weights, *ops)
            value = [here * (c + 0.5 * step_size * d) for c, d in zip(center, change)]
            values.append(value)
            for part in range(2):
                top[row, at - 1, part] = value[part]
    for at in (0, 1):
        for part in range(2):
            top[0, at, part] = jnp.zeros_like(values[0][0])
    weights, here = scalars(ints, roots, rates, slots, 1, slots - 1)
    change = derivative(values[1], values[3], values[1], values[1], values[0], weights, *ops)
    for part in range(2):
        out[0, part] = here * (own[2, part] + step_size * change[part])
    copy = pltpu.make_async_copy(out, out_hbm.at[pl.ds(slots - 1, 1)], sems.at[0])
    copy.start()
    copy.wait()


def stage_kernel(spec, ints, roots, rates, left_ref, right_ref, *refs):
    slots, pieces, lo, hi, first, last = spec
    refs = list(refs)
    own, partner = refs.pop(0), refs.pop(0)
    fars = [[refs.pop(0) for _ in pieces] for _ in range(4)]
    carry = None if first else refs.pop(0)
    top = refs.pop(0) if last else None
    refs.pop(0)
    out_hbm = refs.pop(0)
    carry_out = None if last else refs.pop(0)
    outer, inner, beyond, mid, out, sems, out_sems = refs
    base = max(lo - 2, 0)
    mid_base = max(lo - 3, 0)
    begin, mid_end = max(lo - 1, 0), hi - 1
    out_end = slots - 1 if last else hi - 2
    targets = (outer, inner, beyond)
    near_pair = ints[2] == 1

    def source(group, level):
        for ref, (start, stop) in zip(fars[group], pieces):
            if start <= level < stop:
                return ref.at[level - start]

    def fetch(level):
        at = level - base

        @pl.when(near_pair)
        def _():
            for k, group in enumerate((1, 2, 0)):
                pltpu.make_async_copy(source(group, level), targets[k].at[at], sems.at[at, k]).start()

        @pl.when(jnp.logical_not(near_pair))
        def _():
            for k, group in enumerate((0, 3, 1)):
                pltpu.make_async_copy(source(group, level), targets[k].at[at], sems.at[at, k]).start()

    def arrive(at):
        for k in range(3):
            pltpu.make_async_copy(own.at[0], targets[k].at[at], sems.at[at, k]).wait()

    for level in range(base, hi):
        fetch(level)
    if not first:
        for row in range(3):
            for at in range(2):
                for part in range(2):
                    mid[row, at, part] = carry[row, at, part]
    if last:
        for row in range(3):
            for at in range(2):
                for part in range(2):
                    mid[row, slots - 2 - mid_base + at, part] = top[row, at, part]
    for level in range(base, begin + 1):
        arrive(level - base)
    far_last = hi - 1 - base

    def send(level):
        at = level - base
        return pltpu.make_async_copy(out.at[at], out_hbm.at[level], out_sems.at[at])

    def body(level, with_mid=True):
        ops = left_ref[...], right_ref[...]
        below = jnp.maximum(level - 1, 0)
        at = below - mid_base
        here_mid = [pair(mid, row, at) for row in range(3)]
        down_mid = pair(mid, 1, jnp.maximum(at - 1, 0))
        if with_mid:
            here = level - base
            up_f = jnp.minimum(here + 1, far_last)
            down_f = jnp.maximum(here - 1, 0)
            mine = pair(own, level)
            other = pair(partner, level)
            far = pair(inner, here)
            rows = (
                (far, mine, pair(beyond, here), pair(inner, up_f), pair(inner, down_f)),
                (mine, other, far, pair(own, level + 1), pair(own, below)),
                (other, pair(outer, here), mine, pair(partner, level + 1), pair(partner, below)),
            )
            values = {}
            for row in (1, 0, 2):
                weights, inside = scalars(ints, roots, rates, slots, row, level)
                change = derivative(*rows[row], weights, *ops)
                values[row] = [
                    inside * (c + 0.5 * step_size * d) for c, d in zip(rows[row][0], change)
                ]
            up_mid = values[1]
        else:
            up_mid = pair(mid, 1, at + 1)
        weights, inside = scalars(ints, roots, rates, slots, 1, below)
        change = derivative(here_mid[1], here_mid[2], here_mid[0], up_mid, down_mid, weights, *ops)
        old = pair(own, below)
        for part in range(2):
            out[below - base, part] = inside * (old[part] + step_size * change[part])
        if with_mid:
            for row in range(3):
                for part in range(2):
                    mid[row, level - mid_base, part] = values[row][part]

    def step(level, _):
        @pl.when(level + 1 < hi)
        def _():
            arrive(level + 1 - base)

        body(level)

        @pl.when(level >= 1)
        def _():
            send(level - 1).start()

        return 0

    lax.fori_loop(begin, mid_end, step, 0)
    if last:

        def close(level, _):
            body(level, False)
            send(level - 1).start()
            return 0

        lax.fori_loop(mid_end, slots, close, 0)
    else:
        for row in range(3):
            for at in range(2):
                for part in range(2):
                    carry_out[row, at, part] = mid[row, hi - 3 - mid_base + at, part]
    for level in range(max(lo - 2, 0), out_end):
        send(level).wait()


def specs():
    return (
        pl.BlockSpec(memory_space=pltpu.SMEM),
        pl.BlockSpec(memory_space=pltpu.VMEM),
        pl.BlockSpec(memory_space=pl.ANY),
    )


def top_stage(slots, order, common, own, partner):
    smem, vmem, hbm = specs()
    matrix = (2, order, order)
    return pl.pallas_call(
        functools.partial(top_kernel, slots),
        out_shape=[
            jax.ShapeDtypeStruct((3, 2, *matrix), f32),
            jax.ShapeDtypeStruct((slots, *matrix), f32),
        ],
        in_specs=[smem] * 3 + [vmem] * 4,
        out_specs=[vmem, hbm],
        scratch_shapes=[
            pltpu.VMEM((1, *matrix), f32),
            pltpu.SemaphoreType.DMA((1,)),
        ],
        compiler_params=pltpu.CompilerParams(vmem_limit_bytes=kernel_vmem(slots, order)),
        cost_estimate=pl.CostEstimate(
            flops=5 * 72 * order**3, bytes_accessed=13 * 8 * order**2, transcendentals=0
        ),
        name="top",
    )(*common, own, partner)


def stage(slots, order, cuts, lo, hi, common, own, partner, fars, carry, top, out):
    first, last = lo == 0, hi == slots - 1
    base = max(lo - 2, 0)
    used = [i for i, (a, b) in enumerate(cuts) if b > base and a < hi]
    pieces = [cuts[i] for i in used]
    matrix = (2, order, order)
    operands = [*common, own, partner]
    for group in fars:
        operands += [group[i] for i in used]
    if not first:
        operands.append(carry)
    if last:
        operands.append(top)
    operands.append(out)
    width = hi - base
    mids = (slots if last else hi - 1) - max(lo - 3, 0)
    outs = (slots - 1 if last else hi - 2) - base
    smem, vmem, hbm = specs()
    out_shape = [jax.ShapeDtypeStruct((slots, *matrix), f32)]
    if not last:
        out_shape.append(jax.ShapeDtypeStruct((3, 2, *matrix), f32))
    cells = 4 * (hi - lo)
    count = 4 * len(pieces)
    return pl.pallas_call(
        functools.partial(stage_kernel, (slots, pieces, lo, hi, first, last)),
        out_shape=out_shape,
        in_specs=[smem] * 3
        + [vmem] * 4
        + [vmem] * count
        + [vmem] * (len(operands) - 8 - count)
        + [hbm],
        out_specs=[hbm, vmem][: len(out_shape)],
        scratch_shapes=[
            pltpu.VMEM((width, *matrix), f32),
            pltpu.VMEM((width, *matrix), f32),
            pltpu.VMEM((width, *matrix), f32),
            pltpu.VMEM((3, mids, *matrix), f32),
            pltpu.VMEM((outs, *matrix), f32),
            pltpu.SemaphoreType.DMA((width, 3)),
            pltpu.SemaphoreType.DMA((outs,)),
        ],
        input_output_aliases={len(operands) - 1: 0},
        compiler_params=pltpu.CompilerParams(vmem_limit_bytes=kernel_vmem(slots, order)),
        cost_estimate=pl.CostEstimate(
            flops=cells * 72 * order**3, bytes_accessed=cells * 8 * order**2, transcendentals=0
        ),
        name=f"stage_{lo}",
    )(*operands)


def kernel_vmem(slots, order):
    return (6 * slots + 40) * 8 * order * order


def cut_points(slots):
    top = slots - 1
    points = sorted({0, *[round(top * k / 15) for k in (3, 6, 9)], top - 2, top})
    return list(zip(points[:-1], points[1:]))


def per_device(hierarchy, hamiltonian, couplings, damp_rates, coef_real, coef_imag):
    slots, order = hierarchy.shape[1], hierarchy.shape[-1]
    position = lax.axis_index("na")
    core, side = position % 2, (position // 2) % 2
    toward = 1 - 2 * core
    operators = [0.5 * (m + m.T) for m in (hamiltonian, couplings[0], couplings[1])]
    parts = []
    for m in operators:
        coarse = lax.reduce_precision(m, 8, 7)
        parts.append((coarse.astype(bf16), (m - coarse).astype(bf16)))
    left_ops = jnp.concatenate(
        [jnp.concatenate([p[k] for p in parts], 1) for k in range(2)], 0
    )
    right_ops = jnp.concatenate(
        [jnp.concatenate([p[k] for p in parts], 0) for k in range(2)], 1
    )
    root = jnp.sqrt(jnp.sqrt(coef_real * coef_real + coef_imag * coef_imag))
    rates = jnp.stack([root, coef_real / root, coef_imag / root, damp_rates], 1).reshape(-1)
    counts = np.arange(slots + 2)
    roots = jnp.asarray(np.concatenate([np.sqrt(counts), counts]).astype(np.float32))
    ints = jnp.stack([position, toward, core ^ side, 1 - (core ^ side)]).astype(jnp.int32)
    common = (ints, roots, rates, left_ops, right_ops)
    own = hierarchy[0]
    cuts = cut_points(slots)
    devices = range(slots)
    swap = [(d, d ^ 1) for d in devices]
    partner = lax.ppermute(own, "na", swap)
    pair_far, next_far, pair_near, next_near = [], [], [], []
    for lo, hi in cuts:
        piece = own[lo:hi]
        sent = [d for d in devices if d + lo <= slots - 1 - 2 * (d == 0)]
        if len(pair_far) >= 2:
            piece, _ = lax.optimization_barrier((piece, pair_far[-2]))
        pair = lax.ppermute(piece, "na", [(d, d ^ 2) for d in sent])
        handed = [(d, d + 4) for d in devices if not d & 2 and d + 4 < slots and lo + d + 3 <= slots]
        handed += [(d, d - 4) for d in devices if d & 2 and d >= 4 and lo + d - 2 <= slots - 1]
        pair_far.append(pair)
        pair_near.append(lax.ppermute(pair, "na", swap))
        if handed:
            passed = lax.ppermute(pair, "na", handed)
            next_far.append(passed)
            next_near.append(
                lax.ppermute(passed, "na", swap)
            )
        else:
            next_far.append(jnp.zeros_like(pair))
            next_near.append(jnp.zeros_like(pair))
    fars = (pair_far, next_far, pair_near, next_near)
    bounds = [0] + [hi for _, hi in cuts[1:]]
    top, out = top_stage(slots, order, common, own, partner)
    carry = None
    for lo, hi in zip(bounds[:-1], bounds[1:]):
        results = stage(
            slots, order, cuts, lo, hi, common, own, partner, fars, carry, top, out
        )
        out, carry = results[0], results[-1]
    return out[None]


def solution(mesh):
    in_specs = (
        P(("sweep", "na"), None, None, None, None),
        P(),
        P(),
        P("sweep"),
        P("sweep"),
        P("sweep"),
    )
    out_specs = P(("sweep", "na"), None, None, None, None)
    return jax.shard_map(
        per_device, mesh=mesh, in_specs=in_specs, out_specs=out_specs, check_vma=False
    )
```
